256 devices in a mesh: leaf: 16 (over z, core), list: 16 (over y, x).
Axes of the slice: x: 4, y: 4, z: 8, core: 2. Of those that a mesh axis runs over, the one named last changes fastest.
Arguments:
- panel_charges: bfloat16 [4096, 64, 256], P(('leaf', 'list')), may hold values from -6 to 6
- leaf_basis: bfloat16 [4096, 64, 256], P(('leaf', 'list')), may hold values from -0.375 to 0.375
- near_blocks: bfloat16 [4096, 4, 256, 256], P(('leaf', 'list')), may hold values from -0.1875 to 0.1875
- near_list: int32 [4096, 4], P(('leaf', 'list')), may hold values from 0 to 15, as said below
- far_list: int32 [4096, 8], P(('leaf', 'list')), may hold values from 0 to 255, as said below
- far_count: int32 [4096], P(('leaf', 'list')), may hold values from 1 to 8, as said below
- far_coupling: bfloat16 [4096, 8, 64, 64], P(('leaf', 'list')), may hold values from -0.25 to 0.25
- leaf_transfer: float32 [4096, 64, 64], P(('leaf', 'list')), may hold values from -0.4375 to 0.4375
- device_transfer: float32 [16, 16, 64, 64], P('leaf', 'list'), may hold values from -0.375 to 0.375
- tree_transfer: float32 [24, 64, 64], replicated, may hold values from -0.75 to 0.75
- level_coupling: float32 [28, 4, 64, 64], replicated, may hold values from -0.4375 to 0.4375
Outputs:
- potential: bfloat16 [4096, 64, 256], P(('leaf', 'list'))
The draws below stay inside these ranges and needn't reach their ends.
Inputs may be any that keep to these rules, and one draw needn't show every extreme that they name: `far_list`: each row names 8 different leaves of the leaf's group subtree, none on the leaf's own device; the 16 leaves of one device name, over all their slots, exactly 8 different leaves of each other device of the group. Slots at and after far_count[c] are unused. `near_list`: each row names 4 different leaves of the leaf's own device, the first being the leaf itself.
All inputs are finite; a program needn't handle non-finite values.
Results may differ from the reference program's by a relative error of at most 0.0053.
Values may be sent and summed in bfloat16 or wider, within the bound.
A program may use at most 64 MiB of HBM per device.

```python
import jax
import jax.numpy as jnp
from jax import lax

M = 256
K = 64
R = 64
LEAF_DEV = 16
NFAR = 8
NNEAR = 4
LEAVES = 4096
GROUP = 256
PEER_MOST = 8
TREE_NODES = 24
LEVEL_NODES = 28
N_LEAF = 16
N_LIST = 16


def draw_far_list(key, part):
    block_count = LEAVES // LEAF_DEV
    peer_total = N_LIST - 1
    choose = PEER_MOST
    candidates_count = peer_total * choose
    key_subset = jax.random.fold_in(key, 21)
    key_order = jax.random.fold_in(key, 22)
    column = jnp.arange(LEAF_DEV, dtype=jnp.int32)
    scores = jax.random.randint(key_subset, (block_count, peer_total, LEAF_DEV), 0, 1 << 20, dtype=jnp.int32) * LEAF_DEV + column[None, None, :]
    subset = lax.top_k(scores, choose)[1].astype(jnp.int32)
    own_device = jnp.arange(block_count, dtype=jnp.int32) % N_LIST
    step_ids = jnp.arange(peer_total, dtype=jnp.int32)
    peers = (own_device[:, None] + 1 + step_ids[None, :]) % N_LIST
    candidates = (peers[:, :, None] * LEAF_DEV + subset).reshape(block_count, candidates_count)
    order_scores = jax.random.randint(key_order, (block_count, candidates_count), 0, 1 << 20, dtype=jnp.int32) * candidates_count + jnp.arange(candidates_count, dtype=jnp.int32)[None, :]
    order = jnp.argsort(order_scores, axis=1, stable=True).astype(jnp.int32)
    places = ((jnp.arange(LEAF_DEV, dtype=jnp.int32)[:, None] * NFAR + jnp.arange(NFAR, dtype=jnp.int32)[None, :]) % candidates_count).reshape(-1)
    picked_order = jnp.take(order, places, axis=1)
    result = jnp.take_along_axis(candidates, picked_order, axis=1)
    return result.reshape(LEAVES, NFAR).astype(jnp.int32)


def draw_far_count(key, part):
    block_count = LEAVES // LEAF_DEV
    key_cap = jax.random.fold_in(key, 11)
    key_pick = jax.random.fold_in(key, 12)
    key_each = jax.random.fold_in(key, 13)
    key_spot = jax.random.fold_in(key, 14)
    lowest = max(1, NFAR // 4)
    ceiling = jax.random.randint(key_cap, (block_count,), lowest, NFAR + 1, dtype=jnp.int32)
    chosen = jax.random.randint(key_pick, (), 0, block_count, dtype=jnp.int32)
    ceiling = jnp.where(jnp.arange(block_count, dtype=jnp.int32) == chosen, NFAR, ceiling)
    counts = jax.random.randint(key_each, (block_count, LEAF_DEV), 0, 1 << 20, dtype=jnp.int32) % ceiling[:, None] + 1
    position = jax.random.randint(key_spot, (block_count,), 0, LEAF_DEV, dtype=jnp.int32)
    counts = jnp.where(jnp.arange(LEAF_DEV, dtype=jnp.int32)[None, :] == position[:, None], ceiling[:, None], counts)
    return counts.reshape(LEAVES).astype(jnp.int32)


def draw_near_list(key, part):
    column = jnp.arange(LEAF_DEV, dtype=jnp.int32)
    local_ids = jnp.arange(LEAVES, dtype=jnp.int32) % LEAF_DEV
    scores = jax.random.randint(key, (LEAVES, LEAF_DEV), 0, 1 << 20, dtype=jnp.int32) * LEAF_DEV + column[None, :]
    scores = jnp.where(column[None, :] == local_ids[:, None], 1 << 30, scores)
    return lax.top_k(scores, NNEAR)[1].astype(jnp.int32)


def block_scale(rng, extent, cuts, low, top_value):
    def one(dim, shards_of):
        heights = jax.random.uniform(jax.random.fold_in(jax.random.fold_in(rng, 6), dim), (shards_of,), jnp.float32, low / len(cuts), top_value / len(cuts))
        return jnp.repeat(jnp.exp(heights), extent[dim] // shards_of).reshape((-1,) + (1,) * (len(extent) - dim - 1))

    gain = one(*cuts[0])
    for cut in cuts[1:]:
        gain = gain * one(*cut)
    return gain


def centred(rng, dims, width, most, cuts=(), kind=jnp.bfloat16):
    values = width * jax.random.normal(rng, dims, jnp.float32)
    if cuts:
        values = values * block_scale(rng, dims, cuts, -0.22, 0.18)
    return jnp.clip(values, -most, most).astype(kind)


def setup_inputs(seed: int = 0) -> dict:
    key_list = jax.random.split(jax.random.key(seed), 12)
    panel_charges = centred(key_list[0], (LEAVES, R, M), 1.0, 6.0, ((0, 256),))
    leaf_basis = centred(key_list[1], (LEAVES, K, M), M ** -0.5, 0.375, ((0, 256),))
    near_blocks = centred(key_list[2], (LEAVES, NNEAR, M, M), (M * NNEAR) ** -0.5, 0.1875, ((0, 256),))
    near_list = draw_near_list(jax.random.fold_in(key_list[11], 71), 0)
    far_list = draw_far_list(jax.random.fold_in(key_list[11], 71), 0)
    far_count = draw_far_count(jax.random.fold_in(key_list[11], 71), 0)
    far_coupling = centred(key_list[6], (LEAVES, NFAR, K, K), (K * NFAR) ** -0.5, 0.25, ((0, 256),))
    leaf_transfer = centred(key_list[7], (LEAVES, K, K), (3 * K) ** -0.5, 0.4375, ((0, 256),), jnp.float32)
    device_transfer = centred(key_list[8], (N_LEAF, N_LIST, K, K), (4 * K) ** -0.5, 0.375, ((0, 16), (1, 16)), jnp.float32)
    tree_transfer = centred(key_list[9], (TREE_NODES, K, K), K ** -0.5, 0.75, (), jnp.float32)
    level_coupling = centred(key_list[10], (LEVEL_NODES, 4, K, K), (3 * K) ** -0.5, 0.4375, (), jnp.float32)
    return dict(panel_charges=panel_charges, leaf_basis=leaf_basis, near_blocks=near_blocks, near_list=near_list, far_list=far_list, far_count=far_count, far_coupling=far_coupling, leaf_transfer=leaf_transfer, device_transfer=device_transfer, tree_transfer=tree_transfer, level_coupling=level_coupling)


highest = lax.Precision.HIGHEST
offsets = (-3, -2, 2, 3)


def upper_tree(group_nodes, tree_transfer, level_coupling):
    depth = N_LEAF.bit_length() - 2
    nodes = [group_nodes]
    for height in range(depth - 1):
        current = nodes[-1]
        members = current.shape[0]
        begin_row = 2 * N_LEAF - 2 * members
        product = jnp.einsum('qrb,qba->qra', current, tree_transfer[begin_row:begin_row + members], precision=highest)
        nodes.append(product[0::2] + product[1::2])
    coupled = []
    for height in range(depth):
        current = nodes[height]
        members = current.shape[0]
        begin_row = 2 * N_LEAF - 2 * members
        matrices = level_coupling[begin_row:begin_row + members]
        padded = jnp.pad(current, ((3, 3), (0, 0), (0, 0)))
        parity = jnp.arange(members) % 2
        summed = jnp.zeros_like(current)
        for slot_index, offset in enumerate(offsets):
            source = padded[3 + offset:3 + offset + members]
            contribution = jnp.einsum('qrb,qab->qra', source, matrices[:, slot_index], precision=highest)
            if offset == 3:
                usable = parity == 0
            elif offset == -3:
                usable = parity == 1
            else:
                usable = parity >= 0
            summed = summed + jnp.where(usable[:, None, None], contribution, jnp.zeros((), jnp.float32))
        coupled.append(summed)
    result = coupled[-1]
    for height in reversed(range(depth - 1)):
        members = coupled[height].shape[0]
        begin_row = 2 * N_LEAF - 2 * members
        parent = jnp.repeat(result, 2, axis=0)
        result = coupled[height] + jnp.einsum('qrp,qcp->qrc', parent, tree_transfer[begin_row:begin_row + members], precision=highest)
    return result


def reference(panel_charges, leaf_basis, near_blocks, near_list, far_list, far_count, far_coupling, leaf_transfer, device_transfer, tree_transfer, level_coupling):
    skeleton = jnp.einsum('crm,ckm->crk', panel_charges.astype(jnp.float32), leaf_basis.astype(jnp.float32)).astype(jnp.bfloat16)
    shaped = skeleton.astype(jnp.float32).reshape(N_LEAF, N_LIST, LEAF_DEV, R, K)
    transfer = leaf_transfer.reshape(N_LEAF, N_LIST, LEAF_DEV, K, K)
    device_nodes = jnp.einsum('ljirb,ljiba->ljra', shaped, transfer, precision=highest)
    group_nodes = jnp.einsum('ljrb,ljba->lra', device_nodes, device_transfer, precision=highest)
    top_down = upper_tree(group_nodes, tree_transfer, level_coupling)
    device_down = jnp.einsum('lrp,ljdp->ljrd', top_down, device_transfer, precision=highest)
    from_above = jnp.einsum('ljrd,ljiad->ljira', device_down, transfer, precision=highest).reshape(LEAVES, R, K)
    leaf_ids = jnp.arange(LEAVES, dtype=jnp.int32)
    sources = (leaf_ids // GROUP * GROUP)[:, None] + far_list.astype(jnp.int32)
    usable = jnp.arange(NFAR, dtype=jnp.int32)[None, :] < far_count[:, None]
    picked = jnp.where(usable[:, :, None, None], skeleton[sources], jnp.zeros((), jnp.bfloat16))
    leaf_coupled = jnp.einsum('ckrb,ckab->cra', picked.astype(jnp.float32), far_coupling.astype(jnp.float32))
    coefficients = (leaf_coupled + from_above).astype(jnp.bfloat16)
    far_field = jnp.einsum('crk,ckm->crm', coefficients.astype(jnp.float32), leaf_basis.astype(jnp.float32))
    block_count = LEAVES // LEAF_DEV

    def near_block(inputs):
        charges, blocks, neighbours = inputs
        gathered = charges[neighbours].astype(jnp.float32)
        return jnp.einsum('ckrm,cknm->crn', gathered, blocks.astype(jnp.float32))

    near_field = lax.map(near_block, (panel_charges.reshape(block_count, LEAF_DEV, R, M), near_blocks.reshape(block_count, LEAF_DEV, NNEAR, M, M), near_list.reshape(block_count, LEAF_DEV, NNEAR))).reshape(LEAVES, R, M)
    return (far_field + near_field).astype(jnp.bfloat16)
```

```python
import jax
import jax.numpy as jnp
from jax import lax
from jax.experimental import pallas as pl
from jax.experimental.pallas import tpu as pltpu
from jax.sharding import PartitionSpec as P

MESH = pl.DeviceIdType.MESH
f32, bf16, i32 = jnp.float32, jnp.bfloat16, jnp.int32
SIDE = 4
LIST = 16
LEAF = 16
LEAVES = 16
PAIRS = LEAVES // 2
R = 64
K = 64
M = 256
NFAR = 8
NNEAR = 4
HALF = PAIRS // 2
DEEP = NFAR * 128 + 256
offsets = (-3, -2, 2, 3)
NT = (((1,), (1,)), ((), ()))


def messages():
    q = HALF // 2
    table = [
        ((1, 0), (0, 0), 0, HALF),
        ((-1, 0), (0, 0), 0, HALF),
        ((1, 0), (-1, 0), 0, q),
        ((-1, 0), (1, 0), q, q),
    ]
    for block, begin, count in ((0, 0, HALF), (-1, 0, HALF), (1, 0, HALF), (2, 0, q), (2, q, q)):
        table.append(((0, 1), (block, 0), begin, count))
        table.append(((0, -1), (block, 0), begin, count))
    for block in (0, -1, 1, 2):
        table.append(((0, 1), (block, -1), 0, q))
        table.append(((0, -1), (block, 1), q, q))
    return table


TABLE = messages()
COPIES = len(TABLE)


def split(x):
    high = x.astype(bf16)
    return high, (x - high.astype(f32)).astype(bf16)


def left_half(shape):
    return lax.broadcasted_iota(i32, shape, len(shape) - 1) % 128 < 64


def swap(x):
    return pltpu.roll(x, 64, x.ndim - 1)


def level_of(a, b):
    near_parents = jnp.abs(a // 2 - b // 2) <= 1
    near_grand = jnp.abs(a // 4 - b // 4) <= 1
    return jnp.where(near_parents, 0, jnp.where(near_grand, 1, 2))


def kernel(
    charges_hbm, basis_hbm, near_hbm, nlist_hbm, flist_hbm, fcount_hbm, coup_hbm, lt_hbm, dt_hbm, tt_hbm, lc_hbm,
    out_hbm,
    charges, basis, near, nlist, flist, fcount, coup, lt, dt, tt, lc,
    skel, gup, deep, acc, wtab, wcat, ubd, tsend, rs, zsend, zrecv, ag, out,
    load_sem, near_sem, coup_sem, out_sem, skel_send, skel_recv, rs_send, rs_recv, z_send, z_recv, ag_send, ag_recv,
):
    l = lax.axis_index("leaf")
    j = lax.axis_index("list")
    x, y = j % SIDE, j // SIDE

    loads = [
        pltpu.make_async_copy(charges_hbm, charges, load_sem.at[0]),
        pltpu.make_async_copy(basis_hbm, basis, load_sem.at[1]),
        pltpu.make_async_copy(lt_hbm, lt, load_sem.at[2]),
        pltpu.make_async_copy(dt_hbm.at[0, 0], dt, load_sem.at[3]),
        pltpu.make_async_copy(nlist_hbm, nlist, load_sem.at[4]),
        pltpu.make_async_copy(flist_hbm, flist, load_sem.at[5]),
        pltpu.make_async_copy(fcount_hbm, fcount, load_sem.at[6]),
        pltpu.make_async_copy(tt_hbm.at[l], tt.at[0], load_sem.at[7]),
        pltpu.make_async_copy(tt_hbm.at[LEAF + l // 2], tt.at[1], load_sem.at[8]),
        pltpu.make_async_copy(lc_hbm.at[l], lc.at[0], load_sem.at[9]),
        pltpu.make_async_copy(lc_hbm.at[LEAF + l // 2], lc.at[1], load_sem.at[10]),
        pltpu.make_async_copy(lc_hbm.at[LEAF + LEAF // 2 + l // 4], lc.at[2], load_sem.at[11]),
    ]
    for load in loads:
        load.start()

    def near_copy(c):
        return pltpu.make_async_copy(near_hbm.at[c], near.at[c], near_sem.at[c])

    def coup_copy(c):
        return pltpu.make_async_copy(coup_hbm.at[c], coup.at[c], coup_sem.at[c])

    def out_copy(c):
        return pltpu.make_async_copy(out.at[c], out_hbm.at[c], out_sem.at[c])

    barrier = pltpu.get_barrier_semaphore()

    @pl.loop(1, LIST)
    def _(o):
        pl.semaphore_signal(barrier, inc=1, device_id={"list": (j + o) % LIST}, device_id_type=MESH)

    @pl.loop(1, LEAF)
    def _(o):
        pl.semaphore_signal(barrier, inc=1, device_id={"leaf": (l + o) % LEAF}, device_id_type=MESH)

    @pl.loop(0, LEAVES)
    def _(c):
        near_copy(c).start()
        coup_copy(c).start()

    loads[2].wait()
    loads[3].wait()
    twice = jnp.concatenate([dt[...], dt[...]], axis=1)
    g = jnp.dot(lt[...].reshape(LEAVES * K, K), twice, precision=lax.Precision.HIGHEST)
    g_high, g_low = split(g)
    wide = left_half((LEAVES * K, 128))
    high32, low32 = g_high.astype(f32), g_low.astype(f32)
    gup[...] = jnp.where(wide, high32, low32).astype(bf16)
    deep[:, :, NFAR * 128 : NFAR * 128 + 128] = g_high.reshape(LEAVES, K, 128)
    deep[:, :, NFAR * 128 + 128 :] = jnp.where(wide, low32, 0.0).astype(bf16).reshape(LEAVES, K, 128)

    loads[0].wait()
    loads[1].wait()
    for i in range(PAIRS):
        both = lax.dot_general(
            charges[2 * i : 2 * i + 2].reshape(2 * R, M),
            basis[2 * i : 2 * i + 2].reshape(2 * K, M),
            NT,
            preferred_element_type=f32,
        )
        skel[j * PAIRS + i] = jnp.where(left_half((R, 128)), both[:R], both[R:]).astype(bf16)

    own = jnp.concatenate([skel[j * PAIRS + i] for i in range(PAIRS)], axis=1)
    term = jnp.dot(own, gup[...], preferred_element_type=f32)
    term = term + swap(term)
    for group in range(SIDE):
        rows = term[16 * group : 16 * group + 16]
        tsend[group] = jnp.where(left_half((8, 128)), rows[:8], rows[8:])
    rs[j] = tsend[y]

    pl.semaphore_wait(barrier, LIST + LEAF - 2)

    def rs_copy(o):
        peer = (j + o) % LIST
        return pltpu.make_async_remote_copy(
            src_ref=tsend.at[peer // SIDE],
            dst_ref=rs.at[j],
            send_sem=rs_send.at[o],
            recv_sem=rs_recv.at[o],
            device_id={"list": peer},
            device_id_type=MESH,
        )

    def z_copy(o):
        peer = (l + o) % LEAF
        return pltpu.make_async_remote_copy(
            src_ref=zsend.at[level_of(l, peer)],
            dst_ref=zrecv.at[l],
            send_sem=z_send.at[o],
            recv_sem=z_recv.at[o],
            device_id={"leaf": peer},
            device_id_type=MESH,
        )

    def ag_copy(o):
        return pltpu.make_async_remote_copy(
            src_ref=ag.at[y],
            dst_ref=ag.at[y],
            send_sem=ag_send.at[o],
            recv_sem=ag_recv.at[o],
            device_id={"list": (y + o) % SIDE * SIDE + x},
            device_id_type=MESH,
        )

    def skel_copy(half, index):
        to, block, begin, count = TABLE[index]
        if half:
            to, block = to[::-1], block[::-1]

        def place(at):
            return (y + at[1] + SIDE) % SIDE * SIDE + (x + at[0] + SIDE) % SIDE

        where = skel.at[pl.ds(place(block) * PAIRS + half * HALF + begin, count)]
        return pltpu.make_async_remote_copy(
            src_ref=where,
            dst_ref=where,
            send_sem=skel_send.at[half, index],
            recv_sem=skel_recv.at[half, index],
            device_id={"list": place(to)},
            device_id_type=MESH,
        )

    def send(*indices):
        for index in indices:
            for half in (0, 1):
                skel_copy(half, index).start()

    def receive(*indices):
        for index in indices:
            for half in (0, 1):
                skel_copy(half, index).wait_recv()

    @pl.loop(1, LIST)
    def _(o):
        rs_copy(o).start()

    send(0, 1, 4, 5)

    for load in loads[4:]:
        load.wait()
    first = tt[0]
    second = jnp.dot(first, tt[1], precision=lax.Precision.HIGHEST)
    for h, u in enumerate((None, first, second)):
        for s in range(4):
            matrix = lc[h, s]
            doubled = jnp.concatenate([matrix, matrix], axis=1)
            if h:
                doubled = jnp.dot(u, doubled, precision=lax.Precision.HIGHEST)
            wtab[h * 4 + s] = doubled
    wtab[12] = jnp.zeros((K, 128), f32)

    def table_row(peer):
        h = level_of(l, peer)
        d = jnp.where(h == 0, peer - l, jnp.where(h == 1, peer // 2 - l // 2, peer // 4 - l // 4))
        slot = jnp.where(d < 0, d + 3, d)
        return jnp.where(jnp.abs(peer - l) >= 2, h * 4 + slot, 12)

    square = left_half((K, 128))
    for i in range(LEAF // 2):
        w = jnp.where(square, wtab[table_row(2 * i)], wtab[table_row(2 * i + 1)])
        high, low = split(w)
        wcat[:K, 128 * i : 128 * i + 128] = high
        wcat[K:, 128 * i : 128 * i + 128] = low
    for n, u in enumerate((first, second)):
        doubled = jnp.concatenate([u, u], axis=1)
        block = jnp.concatenate([jnp.where(square, doubled, 0.0), jnp.where(square, 0.0, doubled)], axis=0)
        high, low = split(block)
        ubd[:, 128 * n : 128 * n + 128] = high
        ubd[:, 256 + 128 * n : 256 + 128 * n + 128] = low
    zrecv[l] = jnp.zeros((8, 128), f32)

    def near_leaves(begin, end):
        @pl.loop(begin, end)
        def _(c):
            near_copy(c).wait()
            coup_copy(c).wait()
            total = lax.dot_general(charges[nlist[c, 0]], near[c, 0], NT, preferred_element_type=f32)
            for k in range(1, NNEAR):
                total += lax.dot_general(charges[nlist[c, k]], near[c, k], NT, preferred_element_type=f32)
            acc[c] = total
            for k in range(NFAR):
                matrix = coup[c, k]
                deep[c, :, 128 * k : 128 * k + 128] = jnp.concatenate([matrix, matrix], axis=1)

    near_leaves(0, 5)

    receive(0, 1)
    send(2, 3, 6, 7, 8, 9)
    receive(4, 5)
    send(14, 15)

    @pl.loop(1, LIST)
    def _(o):
        rs_copy(o).wait_recv()

    node = jnp.sum(rs[...], axis=0)
    high, low = split(node)
    product = jnp.dot(jnp.concatenate([high, low], axis=0), ubd[...], preferred_element_type=f32)
    product = product[:8] + product[8:]
    product = product[:, :256] + product[:, 256:]
    zsend[0] = node
    zsend[1] = product[:, :128]
    zsend[2] = product[:, 128:]

    @pl.loop(1, LEAF)
    def _(o):
        z_copy(o).start()

    near_leaves(5, 10)

    receive(2, 3)
    send(10, 11, 12, 13)
    receive(6, 7, 8, 9)
    send(16, 17, 18, 19)

    near_leaves(10, 14)

    @pl.loop(1, LEAF)
    def _(o):
        z_copy(o).wait_recv()

    tops, bottoms = [], []
    narrow = left_half((8, 128))
    for i in range(LEAF // 2):
        even, odd = zrecv[2 * i], zrecv[2 * i + 1]
        tops.append(jnp.where(narrow, even, swap(odd)))
        bottoms.append(jnp.where(narrow, swap(even), odd))
    nodes = jnp.concatenate([jnp.concatenate(tops, axis=1), jnp.concatenate(bottoms, axis=1)], axis=0)
    high, low = split(nodes)
    down = lax.dot_general(jnp.concatenate([high, low], axis=0), wcat[...], NT, preferred_element_type=f32)
    down = down[:16] + down[16:]
    down = down + swap(down)
    ag[y] = jnp.where(narrow, down[:8], down[8:])
    for o in range(1, SIDE):
        ag_copy(o).start()

    receive(10, 13)
    send(20, 21)

    near_leaves(14, 16)

    for o in range(1, SIDE):
        ag_copy(o).wait_recv()
    parts = []
    for group in range(SIDE):
        tile = ag[group]
        other = swap(tile)
        parts += [jnp.where(narrow, tile, other), jnp.where(narrow, other, tile)]
    top_down = jnp.concatenate(parts, axis=0)
    high = top_down.astype(bf16).astype(f32)
    above = jnp.concatenate(
        [
            jnp.where(square, high, top_down - high).astype(bf16),
            jnp.where(square, high, 0.0).astype(bf16),
        ],
        axis=1,
    )

    receive(11, 12, 14, 15, 16, 17, 18, 19, 20, 21)

    lane = lax.broadcasted_iota(i32, (1, 128), 1) // 64

    @pl.loop(0, LEAVES)
    def _(c):
        pieces = []
        for k in range(NFAR):
            source = flist[c, k]
            wanted = jnp.where(k < fcount[c], source % 2, 2)
            keep = jnp.where(lane == wanted, 1.0, 0.0).astype(bf16)
            pieces.append(skel[source // 2] * keep)
        pieces.append(above)
        coefficients = lax.dot_general(jnp.concatenate(pieces, axis=1), deep[c], NT, preferred_element_type=f32).astype(bf16)
        far = jnp.dot(coefficients, basis[c], preferred_element_type=f32)
        out[c] = (far + acc[c]).astype(bf16)
        out_copy(c).start()

    for index in range(COPIES):
        for half in (0, 1):
            skel_copy(half, index).wait_send()

    @pl.loop(1, LIST)
    def _(o):
        rs_copy(o).wait_send()

    @pl.loop(1, LEAF)
    def _(o):
        z_copy(o).wait_send()

    for o in range(1, SIDE):
        ag_copy(o).wait_send()

    @pl.loop(0, LEAVES)
    def _(c):
        out_copy(c).wait()


def on_device(*args):
    anywhere = pl.BlockSpec(memory_space=pl.ANY)
    dma = pltpu.SemaphoreType.DMA
    return pl.pallas_call(
        kernel,
        out_shape=jax.ShapeDtypeStruct((LEAVES, R, M), bf16),
        in_specs=[anywhere] * len(args),
        out_specs=anywhere,
        scratch_shapes=[
            pltpu.VMEM((LEAVES, R, M), bf16),
            pltpu.VMEM((LEAVES, K, M), bf16),
            pltpu.VMEM((LEAVES, NNEAR, M, M), bf16),
            pltpu.SMEM((LEAVES, NNEAR), i32),
            pltpu.SMEM((LEAVES, NFAR), i32),
            pltpu.SMEM((LEAVES,), i32),
            pltpu.VMEM((LEAVES, NFAR, K, K), bf16),
            pltpu.VMEM((LEAVES, K, K), f32),
            pltpu.VMEM((K, K), f32),
            pltpu.VMEM((2, K, K), f32),
            pltpu.VMEM((3, 4, K, K), f32),
            pltpu.VMEM((LIST * PAIRS, R, 128), bf16),
            pltpu.VMEM((LEAVES * K, 128), bf16),
            pltpu.VMEM((LEAVES, K, DEEP), bf16),
            pltpu.VMEM((LEAVES, R, M), f32),
            pltpu.VMEM((13, K, 128), f32),
            pltpu.VMEM((2 * K, LEAF * K), bf16),
            pltpu.VMEM((128, 512), bf16),
            pltpu.VMEM((SIDE, 8, 128), f32),
            pltpu.VMEM((LIST, 8, 128), f32),
            pltpu.VMEM((3, 8, 128), f32),
            pltpu.VMEM((LEAF, 8, 128), f32),
            pltpu.VMEM((SIDE, 8, 128), f32),
            pltpu.VMEM((LEAVES, R, M), bf16),
            dma((12,)),
            dma((LEAVES,)),
            dma((LEAVES,)),
            dma((LEAVES,)),
            dma((2, COPIES)),
            dma((2, COPIES)),
            dma((LIST,)),
            dma((LIST,)),
            dma((LEAF,)),
            dma((LEAF,)),
            dma((SIDE,)),
            dma((SIDE,)),
        ],
        compiler_params=pltpu.CompilerParams(collective_id=0, has_side_effects=True),
        name="h2_product",
    )(*args)


def solution(mesh):
    in_specs = (
        P(("leaf", "list"), None, None),
        P(("leaf", "list"), None, None),
        P(("leaf", "list"), None, None, None),
        P(("leaf", "list"), None),
        P(("leaf", "list"), None),
        P(("leaf", "list")),
        P(("leaf", "list"), None, None, None),
        P(("leaf", "list"), None, None),
        P("leaf", "list", None, None),
        P(),
        P(),
    )
    out_specs = P(("leaf", "list"), None, None)
    return jax.shard_map(on_device, mesh=mesh, in_specs=in_specs, out_specs=out_specs, check_vma=False)
```

```python
import jax
import jax.numpy as jnp
from jax import lax
from jax.experimental import pallas as pl
from jax.experimental.pallas import tpu as pltpu
from jax.sharding import PartitionSpec as P

MESH = pl.DeviceIdType.MESH
f32, bf16, i32 = jnp.float32, jnp.bfloat16, jnp.int32
SIDE = 4
LIST = 16
LEAF = 16
LEAVES = 16
PAIRS = LEAVES // 2
R = 64
K = 64
M = 256
NFAR = 8
NNEAR = 4
HALF = PAIRS // 2
DEEP = NFAR * 128
GROUP = 4
offsets = (-3, -2, 2, 3)
NT = (((1,), (1,)), ((), ()))


def messages():
    q = HALF // 2
    table = [
        ((1, 0), (0, 0), 0, HALF),
        ((-1, 0), (0, 0), 0, HALF),
        ((1, 0), (-1, 0), 0, q),
        ((-1, 0), (1, 0), q, q),
    ]
    for block, begin, count in ((0, 0, HALF), (-1, 0, HALF), (1, 0, HALF), (2, 0, q), (2, q, q)):
        table.append(((0, 1), (block, 0), begin, count))
        table.append(((0, -1), (block, 0), begin, count))
    for block in (0, -1, 1, 2):
        table.append(((0, 1), (block, -1), 0, q))
        table.append(((0, -1), (block, 1), q, q))
    return table


TABLE = messages()
WAVES = ((0, 1), (4, 5), (2, 3), (6, 7, 8, 9), (10, 13), (11, 12, 14, 15, 16, 17, 18, 19, 20, 21))
WAVE_OF = {index: wave for wave, indices in enumerate(WAVES) for index in indices}


def split(x):
    high = x.astype(bf16)
    return high, (x - high.astype(f32)).astype(bf16)


def left_half(shape):
    return lax.broadcasted_iota(i32, shape, len(shape) - 1) % 128 < 64


def swap(x):
    return pltpu.roll(x, 64, x.ndim - 1)


def level_of(a, b):
    near_parents = jnp.abs(a // 2 - b // 2) <= 1
    near_grand = jnp.abs(a // 4 - b // 4) <= 1
    return jnp.where(near_parents, 0, jnp.where(near_grand, 1, 2))


def kernel(
    charges_hbm, basis_hbm, near_hbm, nlist_hbm, flist_hbm, fcount_hbm, coup_hbm, lt_hbm, dt_hbm, tt_hbm, lc_hbm,
    out_hbm,
    charges, basis, near, nlist, flist, fcount, coup, lt, dt, tt, lc,
    skel, gup, gdn, deep, coupled, acc, wtab, wcat, ubd, tsend, rs, zsend, zrecv, ag, out,
    load_sem, near_sem, coup_sem, out_sem, skel_send, skel_recv, rs_send, rs_recv, z_send, z_recv, ag_send, ag_recv,
):
    l = lax.axis_index("leaf")
    j = lax.axis_index("list")
    x, y = j % SIDE, j // SIDE

    barrier = pltpu.get_barrier_semaphore()

    @pl.loop(1, LEAF)
    def _(o):
        pl.semaphore_signal(barrier, inc=1, device_id={"leaf": (l + o) % LEAF}, device_id_type=MESH)

    @pl.loop(1, LIST)
    def _(o):
        pl.semaphore_signal(barrier, inc=1, device_id={"list": (j + o) % LIST}, device_id_type=MESH)

    loads = [
        pltpu.make_async_copy(charges_hbm, charges, load_sem.at[0]),
        pltpu.make_async_copy(basis_hbm, basis, load_sem.at[1]),
        pltpu.make_async_copy(lt_hbm, lt, load_sem.at[2]),
        pltpu.make_async_copy(dt_hbm.at[0, 0], dt, load_sem.at[3]),
        pltpu.make_async_copy(nlist_hbm, nlist, load_sem.at[4]),
        pltpu.make_async_copy(flist_hbm, flist, load_sem.at[5]),
        pltpu.make_async_copy(fcount_hbm, fcount, load_sem.at[6]),
        pltpu.make_async_copy(tt_hbm.at[l], tt.at[0], load_sem.at[7]),
        pltpu.make_async_copy(tt_hbm.at[LEAF + l // 2], tt.at[1], load_sem.at[8]),
        pltpu.make_async_copy(lc_hbm.at[l], lc.at[0], load_sem.at[9]),
        pltpu.make_async_copy(lc_hbm.at[LEAF + l // 2], lc.at[1], load_sem.at[10]),
        pltpu.make_async_copy(lc_hbm.at[LEAF + LEAF // 2 + l // 4], lc.at[2], load_sem.at[11]),
    ]

    def near_copy(group):
        leaves = pl.ds(group * GROUP, GROUP)
        return pltpu.make_async_copy(near_hbm.at[leaves], near.at[leaves], near_sem.at[group])

    coup_copy = pltpu.make_async_copy(coup_hbm, coup, coup_sem)

    for load in loads[:7]:
        load.start()
    for group in range(2):
        near_copy(group).start()
    for load in loads[7:]:
        load.start()
    for group in range(2, LEAVES // GROUP):
        near_copy(group).start()
    coup_copy.start()

    loads[0].wait()
    loads[1].wait()
    for i in range(PAIRS):
        both = lax.dot_general(
            charges[2 * i : 2 * i + 2].reshape(2 * R, M),
            basis[2 * i : 2 * i + 2].reshape(2 * K, M),
            NT,
            preferred_element_type=f32,
        )
        skel[j * PAIRS + i] = jnp.where(left_half((R, 128)), both[:R], both[R:]).astype(bf16)

    loads[2].wait()
    loads[3].wait()
    twice = jnp.concatenate([dt[...], dt[...]], axis=1)
    g = jnp.dot(lt[...].reshape(LEAVES * K, K), twice, precision=lax.Precision.HIGHEST)
    g_high, g_low = split(g)
    wide = left_half((LEAVES * K, 128))
    high32, low32 = g_high.astype(f32), g_low.astype(f32)
    gup[...] = jnp.where(wide, high32, low32).astype(bf16)
    gdn[:, :128] = g_high
    gdn[:, 128:] = jnp.where(wide, low32, 0.0).astype(bf16)

    own = jnp.concatenate([skel[j * PAIRS + i] for i in range(PAIRS)], axis=1)
    term = jnp.dot(own, gup[...], preferred_element_type=f32)
    term = term + swap(term)
    for group in range(SIDE):
        rows = term[16 * group : 16 * group + 16]
        tsend[group] = jnp.where(left_half((8, 128)), rows[:8], rows[8:])
    rs[j] = tsend[y]

    def near_group(group):
        near_copy(group).wait()

        @pl.loop(group * GROUP, group * GROUP + GROUP, step=2)
        def _(first_leaf):
            totals = []
            for c in (first_leaf, first_leaf + 1):
                total = lax.dot_general(charges[nlist[0, c]], near[c, 0], NT, preferred_element_type=f32)
                for k in range(1, NNEAR):
                    total += lax.dot_general(charges[nlist[k, c]], near[c, k], NT, preferred_element_type=f32)
                totals.append(total)
            for n, total in enumerate(totals):
                acc[first_leaf + n] = total

    for load in loads[4:7]:
        load.wait()
    near_group(0)
    near_group(1)

    pl.semaphore_wait(barrier, LIST + LEAF - 2)

    def rs_copy(o):
        peer = (j + o) % LIST
        return pltpu.make_async_remote_copy(
            src_ref=tsend.at[peer // SIDE],
            dst_ref=rs.at[j],
            send_sem=rs_send,
            recv_sem=rs_recv,
            device_id={"list": peer},
            device_id_type=MESH,
        )

    def z_copy(o):
        peer = (l + o) % LEAF
        return pltpu.make_async_remote_copy(
            src_ref=zsend.at[level_of(l, peer)],
            dst_ref=zrecv.at[l],
            send_sem=z_send,
            recv_sem=z_recv,
            device_id={"leaf": peer},
            device_id_type=MESH,
        )

    def ag_copy(o):
        return pltpu.make_async_remote_copy(
            src_ref=ag.at[y],
            dst_ref=ag.at[y],
            send_sem=ag_send,
            recv_sem=ag_recv,
            device_id={"list": (y + o) % SIDE * SIDE + x},
            device_id_type=MESH,
        )

    def skel_copy(half, index):
        to, block, begin, count = TABLE[index]
        if half:
            to, block = to[::-1], block[::-1]

        def place(at):
            return (y + at[1] + SIDE) % SIDE * SIDE + (x + at[0] + SIDE) % SIDE

        where = skel.at[pl.ds(place(block) * PAIRS + half * HALF + begin, count)]
        return pltpu.make_async_remote_copy(
            src_ref=where,
            dst_ref=where,
            send_sem=skel_send,
            recv_sem=skel_recv.at[WAVE_OF[index]],
            device_id={"list": place(to)},
            device_id_type=MESH,
        )

    def send(*indices):
        for index in indices:
            for half in (0, 1):
                skel_copy(half, index).start()

    def all_of(ref, count, send_sem, recv_sem):
        part = ref.at[pl.ds(0, count)]
        return pltpu.make_async_remote_copy(
            src_ref=part,
            dst_ref=part,
            send_sem=send_sem,
            recv_sem=recv_sem,
            device_id={"list": (j + 1) % LIST},
            device_id_type=MESH,
        )

    def receive(*indices):
        wave = WAVES.index(indices)
        count = 2 * sum(TABLE[index][3] for index in indices)
        all_of(skel, count, skel_send, skel_recv.at[wave]).wait_recv()

    rs_all = all_of(rs, LIST - 1, rs_send, rs_recv)
    z_all = all_of(zrecv, LEAF - 1, z_send, z_recv)
    ag_all = all_of(ag, SIDE - 1, ag_send, ag_recv)

    @pl.loop(1, LIST)
    def _(o):
        rs_copy(o).start()

    send(0, 1, 4, 5)

    for load in loads[7:]:
        load.wait()
    first = tt[0]
    second = jnp.dot(first, tt[1], precision=lax.Precision.HIGHEST)
    for h, u in enumerate((None, first, second)):
        for s in range(4):
            matrix = lc[h, s]
            doubled = jnp.concatenate([matrix, matrix], axis=1)
            if h:
                doubled = jnp.dot(u, doubled, precision=lax.Precision.HIGHEST)
            wtab[h * 4 + s] = doubled
    wtab[12] = jnp.zeros((K, 128), f32)

    def table_row(peer):
        h = level_of(l, peer)
        d = jnp.where(h == 0, peer - l, jnp.where(h == 1, peer // 2 - l // 2, peer // 4 - l // 4))
        slot = jnp.where(d < 0, d + 3, d)
        return jnp.where(jnp.abs(peer - l) >= 2, h * 4 + slot, 12)

    square = left_half((K, 128))
    for i in range(LEAF // 2):
        w = jnp.where(square, wtab[table_row(2 * i)], wtab[table_row(2 * i + 1)])
        high, low = split(w)
        wcat[:K, 128 * i : 128 * i + 128] = high
        wcat[K:, 128 * i : 128 * i + 128] = low
    for n, u in enumerate((first, second)):
        doubled = jnp.concatenate([u, u], axis=1)
        block = jnp.concatenate([jnp.where(square, doubled, 0.0), jnp.where(square, 0.0, doubled)], axis=0)
        high, low = split(block)
        ubd[:, 128 * n : 128 * n + 128] = high
        ubd[:, 256 + 128 * n : 256 + 128 * n + 128] = low
    zrecv[l] = jnp.zeros((8, 128), f32)

    near_group(2)

    receive(0, 1)
    send(2, 3, 6, 7, 8, 9)
    receive(4, 5)
    send(14, 15)

    rs_all.wait_recv()

    node = jnp.sum(rs[...], axis=0)
    high, low = split(node)
    product = jnp.dot(jnp.concatenate([high, low], axis=0), ubd[...], preferred_element_type=f32)
    product = product[:8] + product[8:]
    product = product[:, :256] + product[:, 256:]
    zsend[0] = node
    zsend[1] = product[:, :128]
    zsend[2] = product[:, 128:]

    @pl.loop(1, LEAF)
    def _(o):
        z_copy(o).start()

    near_group(3)
    coup_copy.wait()

    @pl.loop(0, LEAVES, step=2)
    def _(first_leaf):
        for c in (first_leaf, first_leaf + 1):
            for k in range(NFAR):
                matrix = coup[c, k]
                deep[c, :, 128 * k : 128 * k + 128] = jnp.concatenate([matrix, matrix], axis=1)

    receive(2, 3)
    send(10, 11, 12, 13)
    receive(6, 7, 8, 9)
    send(16, 17, 18, 19)

    receive(10, 13)
    send(20, 21)

    z_all.wait_recv()

    tops, bottoms = [], []
    narrow = left_half((8, 128))
    for i in range(LEAF // 2):
        even, odd = zrecv[2 * i], zrecv[2 * i + 1]
        tops.append(jnp.where(narrow, even, swap(odd)))
        bottoms.append(jnp.where(narrow, swap(even), odd))
    nodes = jnp.concatenate([jnp.concatenate(tops, axis=1), jnp.concatenate(bottoms, axis=1)], axis=0)
    high, low = split(nodes)
    down = lax.dot_general(jnp.concatenate([high, low], axis=0), wcat[...], NT, preferred_element_type=f32)
    down = down[:16] + down[16:]
    down = down + swap(down)
    ag[y] = jnp.where(narrow, down[:8], down[8:])
    for o in range(1, SIDE):
        ag_copy(o).start()

    receive(11, 12, 14, 15, 16, 17, 18, 19, 20, 21)

    lane = lax.broadcasted_iota(i32, (1, 128), 1) // 64
    pair_mask = left_half((R, 128))

    @pl.loop(0, PAIRS, step=2)
    def _(first_pair):
        results = []
        for i in (first_pair, first_pair + 1):
            rows = []
            for c in (2 * i, 2 * i + 1):
                pieces = []
                for k in range(NFAR):
                    source = flist[k, c]
                    wanted = jnp.where(k < fcount[c], source % 2, 2)
                    keep = jnp.where(lane == wanted, 1.0, 0.0).astype(bf16)
                    pieces.append(skel[source // 2] * keep)
                rows.append(jnp.concatenate(pieces, axis=1))
            both = lax.dot_general(
                jnp.concatenate(rows, axis=0),
                deep[pl.ds(2 * i, 2)].reshape(2 * K, DEEP),
                NT,
                preferred_element_type=f32,
            )
            results.append(jnp.where(pair_mask, both[:R], both[R:]))
        for n, result in enumerate(results):
            coupled[first_pair + n] = result

    ag_all.wait_recv()
    parts = []
    for group in range(SIDE):
        tile = ag[group]
        other = swap(tile)
        parts += [jnp.where(narrow, tile, other), jnp.where(narrow, other, tile)]
    top_down = jnp.concatenate(parts, axis=0)
    high = top_down.astype(bf16).astype(f32)
    above = jnp.concatenate(
        [
            jnp.where(square, high, top_down - high).astype(bf16),
            jnp.where(square, high, 0.0).astype(bf16),
        ],
        axis=1,
    )

    for begin in range(0, PAIRS, 4):
        values = []
        for i in range(begin, begin + 4):
            down_part = lax.dot_general(above, gdn[2 * K * i : 2 * K * i + 2 * K], NT, preferred_element_type=f32)
            coefficients = coupled[i] + down_part
            rows = jnp.concatenate(
                [jnp.where(pair_mask, coefficients, 0.0), jnp.where(pair_mask, 0.0, coefficients)], axis=0
            ).astype(bf16)
            far = jnp.dot(rows, basis[2 * i : 2 * i + 2].reshape(2 * K, M), preferred_element_type=f32)
            values.append((far + acc[2 * i : 2 * i + 2].reshape(2 * R, M)).astype(bf16))
        for n, value in enumerate(values):
            out[2 * (begin + n) : 2 * (begin + n) + 2] = value.reshape(2, R, M)
        leaves = pl.ds(2 * begin, 8)
        pltpu.make_async_copy(out.at[leaves], out_hbm.at[leaves], out_sem).start()

    all_of(skel, (LIST - 1) * PAIRS, skel_send, skel_recv.at[0]).wait_send()
    rs_all.wait_send()
    z_all.wait_send()
    ag_all.wait_send()
    pltpu.make_async_copy(out, out_hbm, out_sem).wait()


def on_device(charges, basis, near, near_list, far_list, *rest):
    args = (charges, basis, near, near_list.T, far_list.T, *rest)
    anywhere = pl.BlockSpec(memory_space=pl.ANY)
    dma = pltpu.SemaphoreType.DMA
    return pl.pallas_call(
        kernel,
        out_shape=jax.ShapeDtypeStruct((LEAVES, R, M), bf16),
        in_specs=[anywhere] * len(args),
        out_specs=anywhere,
        scratch_shapes=[
            pltpu.VMEM((LEAVES, R, M), bf16),
            pltpu.VMEM((LEAVES, K, M), bf16),
            pltpu.VMEM((LEAVES, NNEAR, M, M), bf16),
            pltpu.SMEM((NNEAR, LEAVES), i32),
            pltpu.SMEM((NFAR, LEAVES), i32),
            pltpu.SMEM((LEAVES,), i32),
            pltpu.VMEM((LEAVES, NFAR, K, K), bf16),
            pltpu.VMEM((LEAVES, K, K), f32),
            pltpu.VMEM((K, K), f32),
            pltpu.VMEM((2, K, K), f32),
            pltpu.VMEM((3, 4, K, K), f32),
            pltpu.VMEM((LIST * PAIRS, R, 128), bf16),
            pltpu.VMEM((LEAVES * K, 128), bf16),
            pltpu.VMEM((LEAVES * K, 256), bf16),
            pltpu.VMEM((LEAVES, K, DEEP), bf16),
            pltpu.VMEM((PAIRS, R, 128), f32),
            pltpu.VMEM((LEAVES, R, M), f32),
            pltpu.VMEM((13, K, 128), f32),
            pltpu.VMEM((2 * K, LEAF * K), bf16),
            pltpu.VMEM((128, 512), bf16),
            pltpu.VMEM((SIDE, 8, 128), f32),
            pltpu.VMEM((LIST, 8, 128), f32),
            pltpu.VMEM((3, 8, 128), f32),
            pltpu.VMEM((LEAF, 8, 128), f32),
            pltpu.VMEM((SIDE, 8, 128), f32),
            pltpu.VMEM((LEAVES, R, M), bf16),
            dma((12,)),
            dma((LEAVES // GROUP,)),
            dma(()),
            dma(()),
            dma(()),
            dma((len(WAVES),)),
            dma(()),
            dma(()),
            dma(()),
            dma(()),
            dma(()),
            dma(()),
        ],
        compiler_params=pltpu.CompilerParams(collective_id=0, has_side_effects=True),
        name="h2_product",
    )(*args)


def solution(mesh):
    in_specs = (
        P(("leaf", "list"), None, None),
        P(("leaf", "list"), None, None),
        P(("leaf", "list"), None, None, None),
        P(("leaf", "list"), None),
        P(("leaf", "list"), None),
        P(("leaf", "list")),
        P(("leaf", "list"), None, None, None),
        P(("leaf", "list"), None, None),
        P("leaf", "list", None, None),
        P(),
        P(),
    )
    out_specs = P(("leaf", "list"), None, None)
    return jax.shard_map(on_device, mesh=mesh, in_specs=in_specs, out_specs=out_specs, check_vma=False)
```
